32 devices in a mesh: py: 4 (over y, x), pz: 8 (over z, core).
Axes of the slice: x: 2, y: 2, z: 4, core: 2. Of those that a mesh axis runs over, the one named last changes fastest.
Arguments:
- field_one: float32 [256, 256, 512], P('py', 'pz'), may hold values from -6 to 6
- field_two: float32 [256, 256, 512], P('py', 'pz'), may hold values from -6 to 6
- coef: float32 [2, 2, 8], replicated, may hold values from -4 to 4
Outputs:
- potential_one: float32 [256, 256, 512], P('py', 'pz')
- potential_two: float32 [256, 256, 512], P('py', 'pz')
The draws below stay inside these ranges and needn't reach their ends.
All inputs are finite; a program needn't handle non-finite values.
Results may differ from the reference program's by a relative error of at most 0.00013.
Values sent between devices are 32-bit elements; how exact they have to be, the bound alone decides.
No kernel may reach another device: no remote copies, remote signals or barrier semaphores. Data moves between devices by JAX's collectives and lax.ppermute only.
A program may use at most 256 MiB of HBM per device.

```python
import jax
import jax.numpy as jnp

NX = 512
NY = 256
NZ = 256
BASIS = 8


def block_scale(own_key, dims, cuts, least, high):
    loudness, own = 1.0, jax.random.fold_in(own_key, 6)
    for dim, blocks in cuts:
        draws = jnp.exp(jax.random.uniform(jax.random.fold_in(own, dim), (blocks,), jnp.float32, least / len(cuts), high / len(cuts)))
        loudness = loudness * jnp.repeat(draws, dims[dim] // blocks).reshape([-1 if axis == dim else 1 for axis in range(len(dims))])
    return loudness


def normal_values(own_key, shape, spread, bound, cuts=(), kind=jnp.bfloat16):
    values = jax.random.normal(own_key, shape, jnp.float32) * spread
    if len(cuts) > 0:
        values = block_scale(own_key, shape, cuts, -0.22, 0.18) * values
    return jnp.clip(values, min=-bound, max=bound).astype(kind)


def setup_inputs(seed: int = 0) -> dict:
    splits = jax.random.split(jax.random.key(seed), 4)
    return {
        "field_one": normal_values(splits[0], (NY, NZ, NX), 1.0, 6.0, ((0, 4), (1, 8)), jnp.float32),
        "field_two": normal_values(splits[1], (NY, NZ, NX), 1.0, 6.0, ((0, 4), (1, 8)), jnp.float32),
        "coef": normal_values(splits[2], (2, 2, BASIS), 1.0, 4.0, (), jnp.float32),
    }


def smooth(field):
    for axis in (2, 0, 1):
        field = (4.0 * field + jnp.roll(field, 1, axis) + jnp.roll(field, -1, axis)) / 6.0
    return field

def scaled(length):
    indices = jnp.arange(length, dtype=jnp.int32)
    return jnp.where(indices > length // 2, indices - length, indices).astype(jnp.float32) / length

def reference(field_one, field_two, coef):
    spectra = [jnp.fft.fftn(smooth(field_one)), jnp.fft.fftn(smooth(field_two))]
    scaled_y = scaled(NY)
    scaled_z = scaled(NZ)
    scaled_x = scaled(NX)
    radius = scaled_y[:, None, None] ** 2 + scaled_z[None, :, None] ** 2 + scaled_x[None, None, :] ** 2
    ratio = 4.0 * radius / 3.0
    volume = ratio * jnp.sqrt(ratio)
    outputs = []
    for target in range(2):
        total = jnp.zeros(spectra[0].shape, spectra[0].dtype)
        for index in range(BASIS):
            basis = jnp.exp(-jnp.square((volume - (index + 0.5) / BASIS) * BASIS))
            total = total + basis * (coef[target, 0, index] * spectra[0] + coef[target, 1, index] * spectra[1])
        outputs.append(jnp.real(jnp.fft.ifftn(total)).astype(jnp.float32))
    return (outputs[0], outputs[1])
```

```python
import jax
import jax.numpy as jnp
import numpy as np
from jax import lax
from jax.sharding import PartitionSpec as P

HIGH = lax.Precision.HIGHEST
AXES = ("py", "pz")


def channel_freq(length):
    channel = np.arange(length)
    return np.where(channel == 1, length // 2, channel // 2)


def real_table(length):
    freq = channel_freq(length)
    phase = (freq[:, None] * np.arange(length)[None, :]) % length
    angle = 2.0 * np.pi / length * phase
    odd = (np.arange(length) % 2 == 1) & (np.arange(length) > 1)
    single = np.arange(length) < 2
    table = np.where(odd[:, None], np.sin(angle), np.cos(angle))
    return (table * np.sqrt(np.where(single, 1.0, 2.0) / length)[:, None]).astype(np.float32)


def spline(freq, length):
    return (4.0 + 2.0 * jnp.cos(2.0 * jnp.pi / length * freq.astype(jnp.float32))) / 6.0


def make_kernel(coef, freqs, lengths):
    scaled = [freq.astype(jnp.float32) / length for freq, length in zip(freqs, lengths)]
    ratio = 4.0 * (scaled[0] ** 2 + scaled[1] ** 2 + scaled[2] ** 2) / 3.0
    volume = ratio * jnp.sqrt(ratio)
    smooth = spline(freqs[0], lengths[0]) * spline(freqs[1], lengths[1]) * spline(freqs[2], lengths[2])
    count = coef.shape[2]
    total = [[0.0, 0.0], [0.0, 0.0]]
    for index in range(count):
        basis = jnp.exp(-jnp.square((volume - (index + 0.5) / count) * count))
        for a in range(2):
            for b in range(2):
                total[a][b] = total[a][b] + coef[a, b, index] * basis
    return [[total[a][b] * smooth for b in range(2)] for a in range(2)]


def shards(field_one, field_two, coef):
    y_local, z_local, x_count = field_one.shape
    py_count = lax.axis_size("py")
    pz_count = lax.axis_size("pz")
    y_count = y_local * py_count
    z_count = z_local * pz_count
    world = py_count * pz_count
    per_device = x_count // world
    groups = min(2, per_device)
    rows = per_device // groups
    fields = (field_one, field_two)
    x_table = real_table(x_count).reshape(world, groups, rows, x_count)
    y_table = jnp.asarray(real_table(y_count))
    z_table = jnp.asarray(real_table(z_count))
    me = lax.axis_index("py") * pz_count + lax.axis_index("pz")
    freq_y = jnp.asarray(channel_freq(y_count))
    freq_z = jnp.asarray(channel_freq(z_count))

    arrived = []
    for group in range(groups):
        table = jnp.asarray(x_table[:, group].reshape(world * rows, x_count))
        pair = []
        for field in fields:
            spectrum = jnp.einsum("qx,yzx->qyz", table, field, precision=HIGH)
            spectrum = spectrum.reshape(world, rows, y_local * z_local)
            pair.append(lax.all_to_all(spectrum, AXES, split_axis=0, concat_axis=0, tiled=True))
        arrived.append(pair)

    sent_back = []
    for group in range(groups):
        channel = me * per_device + group * rows + jnp.arange(rows)
        freq_x = jnp.where(channel == 1, x_count // 2, channel // 2)
        kernel = make_kernel(
            coef,
            (freq_y[None, :, None], freq_z[None, None, :], freq_x[:, None, None]),
            (y_count, z_count, x_count),
        )
        spectra = []
        for value in arrived[group]:
            value = value.reshape(py_count, pz_count, rows, y_local, z_local)
            value = value.transpose(2, 0, 3, 1, 4).reshape(rows, y_count, z_count)
            value = jnp.einsum("ryz,mz->rym", value, z_table, precision=HIGH)
            spectra.append(jnp.einsum("rym,ky->rkm", value, y_table, precision=HIGH))
        pair = []
        for a in range(2):
            value = kernel[a][0] * spectra[0] + kernel[a][1] * spectra[1]
            value = jnp.einsum("rkm,ky->rym", value, y_table, precision=HIGH)
            value = jnp.einsum("rym,mz->ryz", value, z_table, precision=HIGH)
            value = value.reshape(rows, py_count, y_local, pz_count, z_local).transpose(1, 3, 0, 2, 4)
            value = value.reshape(world, rows, y_local * z_local)
            pair.append(lax.all_to_all(value, AXES, split_axis=0, concat_axis=0, tiled=True))
        sent_back.append(pair)

    results = []
    for a in range(2):
        total = None
        for group in range(groups):
            table = jnp.asarray(x_table[:, group].reshape(world * rows, x_count))
            value = sent_back[group][a].reshape(world * rows, y_local, z_local)
            part = jnp.einsum("qyz,qx->yzx", value, table, precision=HIGH)
            total = part if total is None else total + part
        results.append(total)
    return tuple(results)


def solution(mesh):
    in_specs = (P("py", "pz", None), P("py", "pz", None), P())
    out_specs = (P("py", "pz", None), P("py", "pz", None))
    return jax.shard_map(shards, mesh=mesh, in_specs=in_specs, out_specs=out_specs, check_vma=False)
```

```python
import functools

import jax
import jax.numpy as jnp
import numpy as np
from jax import lax
from jax.experimental import pallas as pl
from jax.experimental.pallas import tpu as pltpu
from jax.sharding import PartitionSpec as P

HIGH = lax.Precision.HIGHEST
AXES = ("py", "pz")
LANES = 128
SUBLANES = 8
VMEM_LIMIT = 56 * 1024 * 1024


def channel_freq(length):
    channel = np.arange(length)
    return np.where(channel == 1, length // 2, channel // 2)


def real_table(length):
    freq = channel_freq(length)
    phase = (freq[:, None] * np.arange(length)[None, :]) % length
    angle = 2.0 * np.pi / length * phase
    odd = (np.arange(length) % 2 == 1) & (np.arange(length) > 1)
    single = np.arange(length) < 2
    table = np.where(odd[:, None], np.sin(angle), np.cos(angle))
    return (table * np.sqrt(np.where(single, 1.0, 2.0) / length)[:, None]).astype(np.float32)


def spline(freq, length):
    return (4.0 + 2.0 * jnp.cos(2.0 * jnp.pi / length * freq.astype(jnp.float32))) / 6.0


def make_kernel(coef, freqs, lengths):
    scaled = [freq.astype(jnp.float32) / length for freq, length in zip(freqs, lengths)]
    ratio = 4.0 * (scaled[0] ** 2 + scaled[1] ** 2 + scaled[2] ** 2) / 3.0
    volume = ratio * jnp.sqrt(ratio)
    smooth = spline(freqs[0], lengths[0]) * spline(freqs[1], lengths[1]) * spline(freqs[2], lengths[2])
    count = coef.shape[2]
    total = [[0.0, 0.0], [0.0, 0.0]]
    for index in range(count):
        basis = jnp.exp(-jnp.square((volume - (index + 0.5) / count) * count))
        for a in range(2):
            for b in range(2):
                total[a][b] = total[a][b] + coef[a, b, index] * basis
    return [total[a][b] * smooth for a in range(2) for b in range(2)]


def dot(left, right, left_dim, right_dim):
    dims = (((left_dim,), (right_dim,)), ((), ()))
    return lax.dot_general(left, right, dims, precision=HIGH, preferred_element_type=jnp.float32)


def params():
    return pltpu.CompilerParams(vmem_limit_bytes=VMEM_LIMIT)


def x_forward_body(table_ref, one_ref, two_ref, out_ref):
    world, _, rows, cells = out_ref.shape
    for a, ref in enumerate((one_ref, two_ref)):
        values = ref[...].reshape(cells, ref.shape[-1])
        out_ref[:, a] = dot(table_ref[...], values, 1, 1).reshape(world, rows, cells)


def cell_blocks(y_local, z_local):
    blocks = 4
    while y_local % blocks or (y_local // blocks * z_local) % LANES:
        blocks //= 2
    return blocks


def x_forward(table, fields, world, rows):
    y_local, z_local, x_count = fields[0].shape
    blocks = cell_blocks(y_local, z_local)
    part = y_local // blocks
    field_spec = pl.BlockSpec((part, z_local, x_count), lambda i: (i, 0, 0))
    return pl.pallas_call(
        x_forward_body,
        grid=(blocks,),
        in_specs=[pl.BlockSpec(table.shape, lambda i: (0, 0)), field_spec, field_spec],
        out_specs=pl.BlockSpec((world, 2, rows, part * z_local), lambda i: (0, 0, 0, i)),
        out_shape=jax.ShapeDtypeStruct((world, 2, rows, y_local * z_local), jnp.float32),
        compiler_params=params(),
        name="x_forward",
    )(table, *fields)


def x_inverse_body(table_ref, value_ref, *refs):
    outs = refs[-2:]
    for a, out_ref in enumerate(outs):
        world, _, rows, cells = value_ref.shape
        value = value_ref[:, a].reshape(world * rows, cells)
        total = dot(value, table_ref[...], 0, 0).reshape(out_ref.shape)
        out_ref[...] = total if len(refs) == 2 else refs[a][...] + total


def x_inverse(table, value, before, y_local, z_local):
    world, _, rows, cells = value.shape
    x_count = table.shape[1]
    blocks = cell_blocks(y_local, z_local)
    part = y_local // blocks
    field_spec = pl.BlockSpec((part, z_local, x_count), lambda i: (i, 0, 0))
    out = jax.ShapeDtypeStruct((y_local, z_local, x_count), jnp.float32)
    return pl.pallas_call(
        x_inverse_body,
        grid=(blocks,),
        in_specs=[
            pl.BlockSpec(table.shape, lambda i: (0, 0)),
            pl.BlockSpec((world, 2, rows, part * z_local), lambda i: (0, 0, 0, i)),
        ]
        + [field_spec] * len(before),
        out_specs=(field_spec, field_spec),
        out_shape=(out, out),
        compiler_params=params(),
        name="x_inverse",
    )(table, value, *before)


def swap_groups(values, width):
    values = list(values)
    count = len(values)
    lane = lax.broadcasted_iota(jnp.int32, values[0].shape, 1)
    step = 1
    while step < count:
        low = (lane // (step * width)) % 2 == 0
        for m in range(count):
            if m & step == 0:
                one, two = values[m], values[m | step]
                values[m] = jnp.where(low, one, pltpu.roll(two, step * width, 1))
                values[m | step] = jnp.where(low, pltpu.roll(one, LANES - step * width, 1), two)
        step *= 2
    return values


def yz_body(value_ref, y_ref, z_ref, k00, k01, k10, k11, out_ref, scratch):
    py, pz, _, rows, cells = value_ref.shape
    y_count = y_ref.shape[0]
    z_count = z_ref.shape[0]
    z_local = z_count // pz
    split = LANES // z_local
    tiles = cells // LANES
    block = split * tiles * rows
    halves = z_count // LANES
    r = pl.program_id(0)

    @pl.when(r == 0)
    def _():
        for a in range(2):

            def forward(i, carry):
                spread = []
                for high in range(pz // split):
                    group = []
                    for low in range(split):
                        value = value_ref[i, high * split + low, a]
                        group.append(
                            jnp.concatenate([value[:, t * LANES : (t + 1) * LANES] for t in range(tiles)], axis=0)
                        )
                    spread.append(swap_groups(group, z_local))
                lines = [jnp.concatenate([part[p] for part in spread], axis=1) for p in range(split)]
                lines = jnp.concatenate(lines, axis=0)
                lines = dot(lines, z_ref[...], 1, 1)
                for t in range(halves):
                    scratch[a, t, pl.ds(i * block, block), :] = lines[:, t * LANES : (t + 1) * LANES]
                return carry

            lax.fori_loop(0, py, forward, 0)

    spectra = []
    for a in range(2):
        plane = [scratch[a, t, pl.ds(r, y_count, stride=rows), :] for t in range(halves)]
        spectra.append(dot(y_ref[...], jnp.concatenate(plane, axis=1), 1, 0))
    for a, (first, second) in enumerate(((k00, k01), (k10, k11))):
        weighed = first[0] * spectra[0] + second[0] * spectra[1]
        plane = dot(y_ref[...], weighed, 0, 0)
        for t in range(halves):
            scratch[a, t, pl.ds(r, y_count, stride=rows), :] = plane[:, t * LANES : (t + 1) * LANES]

    @pl.when(r == rows - 1)
    def _():
        for a in range(2):

            def backward(i, carry):
                lines = [scratch[a, t, pl.ds(i * block, block), :] for t in range(halves)]
                lines = dot(jnp.concatenate(lines, axis=1), z_ref[...], 1, 0)
                size = block // split
                for high in range(pz // split):
                    lanes = slice(high * LANES, (high + 1) * LANES)
                    group = swap_groups([lines[p * size : (p + 1) * size, lanes] for p in range(split)], z_local)
                    for low in range(split):
                        for t in range(tiles):
                            piece = group[low][t * rows : (t + 1) * rows]
                            out_ref[i, high * split + low, a, :, t * LANES : (t + 1) * LANES] = piece
                return carry

            lax.fori_loop(0, py, backward, 0)


def yz_apply(value, kernel, sizes):
    py, pz, y_local, z_local = sizes
    _, _, rows, cells = value.shape
    y_count, z_count = py * y_local, pz * z_local
    y_table, z_table = real_table(y_count), jnp.asarray(real_table(z_count))
    value = value.reshape(py, pz, 2, rows, cells)
    if rows % SUBLANES or LANES % z_local or cells % LANES or z_count % LANES or pz % (LANES // z_local):
        return yz_plain(value, kernel, sizes, jnp.asarray(y_table), z_table)
    split = LANES // z_local
    order = np.arange(y_count).reshape(py, y_local // split, split).transpose(0, 2, 1).reshape(-1)
    y_table = jnp.asarray(y_table[:, order])
    whole = lambda shape: pl.BlockSpec(shape, lambda r: (0,) * len(shape))
    k_spec = pl.BlockSpec((1, y_count, z_count), lambda r: (r, 0, 0))
    out = pl.pallas_call(
        yz_body,
        grid=(rows,),
        in_specs=[whole(value.shape), whole(y_table.shape), whole(z_table.shape)] + [k_spec] * 4,
        out_specs=whole(value.shape),
        out_shape=jax.ShapeDtypeStruct(value.shape, jnp.float32),
        scratch_shapes=[pltpu.VMEM((2, z_count // LANES, y_count * rows, LANES), jnp.float32)],
        compiler_params=params(),
        name="yz_apply",
    )(value, y_table, z_table, *kernel)
    return out.reshape(py * pz, 2, rows, cells)


def yz_plain(value, kernel, sizes, y_table, z_table):
    py, pz, y_local, z_local = sizes
    rows = value.shape[3]
    value = value.reshape(py, pz, 2, rows, y_local, z_local).transpose(2, 3, 0, 4, 1, 5)
    value = value.reshape(2, rows, py * y_local, pz * z_local)
    value = jnp.einsum("aryz,mz->arym", value, z_table, precision=HIGH)
    value = jnp.einsum("arym,ky->arkm", value, y_table, precision=HIGH)
    k00, k01, k10, k11 = kernel
    value = jnp.stack([k00 * value[0] + k01 * value[1], k10 * value[0] + k11 * value[1]])
    value = jnp.einsum("arkm,ky->arym", value, y_table, precision=HIGH)
    value = jnp.einsum("arym,mz->aryz", value, z_table, precision=HIGH)
    value = value.reshape(2, rows, py, y_local, pz, z_local).transpose(2, 4, 0, 1, 3, 5)
    return value.reshape(py * pz, 2, rows, y_local * z_local)


def shards(field_one, field_two, coef):
    y_local, z_local, x_count = field_one.shape
    py_count = lax.axis_size("py")
    pz_count = lax.axis_size("pz")
    sizes = (py_count, pz_count, y_local, z_local)
    y_count = y_local * py_count
    z_count = z_local * pz_count
    world = py_count * pz_count
    per_device = x_count // world
    groups = 2 if per_device % (2 * SUBLANES) == 0 else 1
    rows = per_device // groups
    x_table = real_table(x_count).reshape(world, groups, rows, x_count)
    tables = [jnp.asarray(x_table[:, g].reshape(world * rows, x_count)) for g in range(groups)]
    me = lax.axis_index("py") * pz_count + lax.axis_index("pz")
    freq_y = jnp.asarray(channel_freq(y_count))
    freq_z = jnp.asarray(channel_freq(z_count))

    def exchange(value):
        return lax.all_to_all(value, AXES, split_axis=0, concat_axis=0, tiled=True)

    arrived = []
    for group in range(groups):
        arrived.append(exchange(x_forward(tables[group], (field_one, field_two), world, rows)))
    returned = []
    for group in range(groups):
        channel = me * per_device + group * rows + jnp.arange(rows)
        freq_x = jnp.where(channel == 1, x_count // 2, channel // 2)
        kernel = make_kernel(
            coef,
            (freq_y[None, :, None], freq_z[None, None, :], freq_x[:, None, None]),
            (y_count, z_count, x_count),
        )
        returned.append(exchange(yz_apply(arrived[group], kernel, sizes)))
    results = ()
    for group in range(groups):
        results = x_inverse(tables[group], returned[group], results, y_local, z_local)
    return tuple(results)


def solution(mesh):
    in_specs = (P("py", "pz", None), P("py", "pz", None), P())
    out_specs = (P("py", "pz", None), P("py", "pz", None))
    return jax.shard_map(shards, mesh=mesh, in_specs=in_specs, out_specs=out_specs, check_vma=False)
```

```python
import functools

import jax
import jax.numpy as jnp
import numpy as np
from jax import lax
from jax.experimental import pallas as pl
from jax.experimental.pallas import tpu as pltpu
from jax.sharding import PartitionSpec as P

HIGH = lax.Precision.HIGHEST
AXES = ("py", "pz")
LANES = 128
SUBLANES = 8
BLOCKS = 2
VMEM_LIMIT = 56 * 1024 * 1024


def channel_freq(length):
    channel = np.arange(length)
    return np.where(channel == 1, length // 2, channel // 2)


def real_table(length):
    freq = channel_freq(length)
    phase = (freq[:, None] * np.arange(length)[None, :]) % length
    angle = 2.0 * np.pi / length * phase
    odd = (np.arange(length) % 2 == 1) & (np.arange(length) > 1)
    single = np.arange(length) < 2
    table = np.where(odd[:, None], np.sin(angle), np.cos(angle))
    return (table * np.sqrt(np.where(single, 1.0, 2.0) / length)[:, None]).astype(np.float32)


def spline(freq, length):
    return (4.0 + 2.0 * jnp.cos(2.0 * jnp.pi / length * freq.astype(jnp.float32))) / 6.0


def make_kernel(coef, freqs, lengths):
    scaled = [freq.astype(jnp.float32) / length for freq, length in zip(freqs, lengths)]
    ratio = 4.0 * (scaled[0] ** 2 + scaled[1] ** 2 + scaled[2] ** 2) / 3.0
    volume = ratio * jnp.sqrt(ratio)
    smooth = spline(freqs[0], lengths[0]) * spline(freqs[1], lengths[1]) * spline(freqs[2], lengths[2])
    count = coef.shape[2]
    total = [[0.0, 0.0], [0.0, 0.0]]
    for index in range(count):
        basis = jnp.exp(-jnp.square((volume - (index + 0.5) / count) * count))
        for a in range(2):
            for b in range(2):
                total[a][b] = total[a][b] + coef[a, b, index] * basis
    return [total[a][b] * smooth for a in range(2) for b in range(2)]


def dot(left, right, left_dim, right_dim):
    dims = (((left_dim,), (right_dim,)), ((), ()))
    return lax.dot_general(left, right, dims, precision=HIGH, preferred_element_type=jnp.float32)


def params():
    return pltpu.CompilerParams(vmem_limit_bytes=VMEM_LIMIT)


def x_groups(x_count, world):
    table, freq = real_table(x_count), channel_freq(x_count)
    if x_count // world % (2 * SUBLANES) or x_count // 2 % LANES:
        return [(table, 0, freq)]
    half = x_count // 2
    return [(table[freq % 2 == odd][:, :half], 1 - 2 * odd, freq[freq % 2 == odd]) for odd in range(2)]


def x_forward_body(sign, table_ref, one_ref, two_ref, out_ref):
    world, _, rows, cells = out_ref.shape
    for a, ref in enumerate((one_ref, two_ref)):
        values = ref[...].reshape(cells, ref.shape[-1])
        if sign:
            half = values.shape[1] // 2
            values = values[:, :half] + values[:, half:] if sign > 0 else values[:, :half] - values[:, half:]
        out_ref[:, a] = dot(table_ref[...], values, 1, 1).reshape(world, rows, cells)


def cell_blocks(y_local, z_local):
    blocks = BLOCKS
    while y_local % blocks or (y_local // blocks * z_local) % LANES:
        blocks //= 2
    return blocks


def x_forward(table, sign, fields, world):
    y_local, z_local, x_count = fields[0].shape
    rows = table.shape[0] // world
    blocks = cell_blocks(y_local, z_local)
    part = y_local // blocks
    field_spec = pl.BlockSpec((part, z_local, x_count), lambda i: (i, 0, 0))
    return pl.pallas_call(
        functools.partial(x_forward_body, sign),
        grid=(blocks,),
        in_specs=[pl.BlockSpec(table.shape, lambda i: (0, 0)), field_spec, field_spec],
        out_specs=pl.BlockSpec((world, 2, rows, part * z_local), lambda i: (0, 0, 0, i)),
        out_shape=jax.ShapeDtypeStruct((world, 2, rows, y_local * z_local), jnp.float32),
        compiler_params=params(),
        name="x_forward",
    )(table, *fields)


def x_inverse_body(table_ref, value_ref, *refs):
    for a, out_ref in enumerate(refs[-2:]):
        world, _, rows, cells = value_ref.shape
        value = value_ref[:, a].reshape(world * rows, cells)
        total = dot(value, table_ref[...], 0, 0)
        if len(refs) == 4:
            even = refs[a][...].reshape(total.shape)
            total = jnp.concatenate([even + total, even - total], axis=1)
        out_ref[...] = total.reshape(out_ref.shape)


def x_inverse(table, value, even, y_local, z_local):
    world, _, rows, cells = value.shape
    width = table.shape[1]
    blocks = cell_blocks(y_local, z_local)
    part = y_local // blocks
    block = lambda count: pl.BlockSpec((part, z_local, count), lambda i: (i, 0, 0))
    x_count = 2 * width if even else width
    out = jax.ShapeDtypeStruct((y_local, z_local, x_count), jnp.float32)
    return pl.pallas_call(
        x_inverse_body,
        grid=(blocks,),
        in_specs=[
            pl.BlockSpec(table.shape, lambda i: (0, 0)),
            pl.BlockSpec((world, 2, rows, part * z_local), lambda i: (0, 0, 0, i)),
        ]
        + [block(width)] * len(even),
        out_specs=(block(x_count), block(x_count)),
        out_shape=(out, out),
        compiler_params=params(),
        name="x_inverse",
    )(table, value, *even)


def swap_groups(values, width):
    values = list(values)
    count = len(values)
    lane = lax.broadcasted_iota(jnp.int32, values[0].shape, 1)
    step = 1
    while step < count:
        low = (lane // (step * width)) % 2 == 0
        for m in range(count):
            if m & step == 0:
                one, two = values[m], values[m | step]
                values[m] = jnp.where(low, one, pltpu.roll(two, step * width, 1))
                values[m | step] = jnp.where(low, pltpu.roll(one, LANES - step * width, 1), two)
        step *= 2
    return values


def yz_body(value_ref, y_ref, z_ref, k00, k01, k10, k11, out_ref, scratch):
    py, pz, _, rows, cells = value_ref.shape
    y_count = y_ref.shape[0]
    z_count = z_ref.shape[0]
    z_local = z_count // pz
    split = LANES // z_local
    tiles = cells // LANES
    block = split * tiles * rows
    halves = z_count // LANES
    r = pl.program_id(0)

    @pl.when(r == 0)
    def _():
        for a in range(2):

            def forward(i, carry):
                spread = []
                for high in range(pz // split):
                    group = []
                    for low in range(split):
                        value = value_ref[i, high * split + low, a]
                        group.append(
                            jnp.concatenate([value[:, t * LANES : (t + 1) * LANES] for t in range(tiles)], axis=0)
                        )
                    spread.append(swap_groups(group, z_local))
                lines = [jnp.concatenate([part[p] for part in spread], axis=1) for p in range(split)]
                lines = jnp.concatenate(lines, axis=0)
                lines = dot(lines, z_ref[...], 1, 1)
                for t in range(halves):
                    scratch[a, t, pl.ds(i * block, block), :] = lines[:, t * LANES : (t + 1) * LANES]
                return carry

            lax.fori_loop(0, py, forward, 0)

    spectra = []
    for a in range(2):
        plane = [scratch[a, t, pl.ds(r, y_count, stride=rows), :] for t in range(halves)]
        spectra.append(dot(y_ref[...], jnp.concatenate(plane, axis=1), 1, 0))
    for a, (first, second) in enumerate(((k00, k01), (k10, k11))):
        weighed = first[0] * spectra[0] + second[0] * spectra[1]
        plane = dot(y_ref[...], weighed, 0, 0)
        for t in range(halves):
            scratch[a, t, pl.ds(r, y_count, stride=rows), :] = plane[:, t * LANES : (t + 1) * LANES]

    @pl.when(r == rows - 1)
    def _():
        for a in range(2):

            def backward(i, carry):
                lines = [scratch[a, t, pl.ds(i * block, block), :] for t in range(halves)]
                lines = dot(jnp.concatenate(lines, axis=1), z_ref[...], 1, 0)
                size = block // split
                for high in range(pz // split):
                    lanes = slice(high * LANES, (high + 1) * LANES)
                    group = swap_groups([lines[p * size : (p + 1) * size, lanes] for p in range(split)], z_local)
                    for low in range(split):
                        for t in range(tiles):
                            piece = group[low][t * rows : (t + 1) * rows]
                            out_ref[i, high * split + low, a, :, t * LANES : (t + 1) * LANES] = piece
                return carry

            lax.fori_loop(0, py, backward, 0)


def yz_apply(value, kernel, sizes):
    py, pz, y_local, z_local = sizes
    _, _, rows, cells = value.shape
    y_count, z_count = py * y_local, pz * z_local
    y_table, z_table = real_table(y_count), jnp.asarray(real_table(z_count))
    value = value.reshape(py, pz, 2, rows, cells)
    if rows % SUBLANES or LANES % z_local or cells % LANES or z_count % LANES or pz % (LANES // z_local):
        return yz_plain(value, kernel, sizes, jnp.asarray(y_table), z_table)
    split = LANES // z_local
    order = np.arange(y_count).reshape(py, y_local // split, split).transpose(0, 2, 1).reshape(-1)
    y_table = jnp.asarray(y_table[:, order])
    whole = lambda shape: pl.BlockSpec(shape, lambda r: (0,) * len(shape))
    k_spec = pl.BlockSpec((1, y_count, z_count), lambda r: (r, 0, 0))
    out = pl.pallas_call(
        yz_body,
        grid=(rows,),
        in_specs=[whole(value.shape), whole(y_table.shape), whole(z_table.shape)] + [k_spec] * 4,
        out_specs=whole(value.shape),
        out_shape=jax.ShapeDtypeStruct(value.shape, jnp.float32),
        scratch_shapes=[pltpu.VMEM((2, z_count // LANES, y_count * rows, LANES), jnp.float32)],
        compiler_params=params(),
        name="yz_apply",
    )(value, y_table, z_table, *kernel)
    return out.reshape(py * pz, 2, rows, cells)


def yz_plain(value, kernel, sizes, y_table, z_table):
    py, pz, y_local, z_local = sizes
    rows = value.shape[3]
    value = value.reshape(py, pz, 2, rows, y_local, z_local).transpose(2, 3, 0, 4, 1, 5)
    value = value.reshape(2, rows, py * y_local, pz * z_local)
    value = jnp.einsum("aryz,mz->arym", value, z_table, precision=HIGH)
    value = jnp.einsum("arym,ky->arkm", value, y_table, precision=HIGH)
    k00, k01, k10, k11 = kernel
    value = jnp.stack([k00 * value[0] + k01 * value[1], k10 * value[0] + k11 * value[1]])
    value = jnp.einsum("arkm,ky->arym", value, y_table, precision=HIGH)
    value = jnp.einsum("arym,mz->aryz", value, z_table, precision=HIGH)
    value = value.reshape(2, rows, py, y_local, pz, z_local).transpose(2, 4, 0, 1, 3, 5)
    return value.reshape(py * pz, 2, rows, y_local * z_local)


def shards(field_one, field_two, coef):
    y_local, z_local, x_count = field_one.shape
    py_count = lax.axis_size("py")
    pz_count = lax.axis_size("pz")
    sizes = (py_count, pz_count, y_local, z_local)
    y_count = y_local * py_count
    z_count = z_local * pz_count
    world = py_count * pz_count
    me = lax.axis_index("py") * pz_count + lax.axis_index("pz")
    freq_y = jnp.asarray(channel_freq(y_count))
    freq_z = jnp.asarray(channel_freq(z_count))
    groups = [(jnp.asarray(table), sign, freq) for table, sign, freq in x_groups(x_count, world)]

    def exchange(value):
        return lax.all_to_all(value, AXES, split_axis=0, concat_axis=0, tiled=True)

    arrived = [exchange(x_forward(table, sign, (field_one, field_two), world)) for table, sign, _ in groups]
    returned = []
    for value, (_, _, freq) in zip(arrived, groups):
        rows = freq.size // world
        freq_x = lax.dynamic_slice_in_dim(jnp.asarray(freq), me * rows, rows)
        kernel = make_kernel(
            coef,
            (freq_y[None, :, None], freq_z[None, None, :], freq_x[:, None, None]),
            (y_count, z_count, x_count),
        )
        returned.append(exchange(yz_apply(value, kernel, sizes)))
    results = ()
    for value, (table, _, _) in zip(returned, groups):
        results = x_inverse(table, value, results, y_local, z_local)
    return tuple(results)


def solution(mesh):
    in_specs = (P("py", "pz", None), P("py", "pz", None), P())
    out_specs = (P("py", "pz", None), P("py", "pz", None))
    return jax.shard_map(shards, mesh=mesh, in_specs=in_specs, out_specs=out_specs, check_vma=False)
```

```python
import functools

import jax
import jax.numpy as jnp
import numpy as np
from jax import lax
from jax.experimental import pallas as pl
from jax.experimental.pallas import tpu as pltpu
from jax.sharding import PartitionSpec as P


HIGH = lax.Precision.HIGHEST
AXES = ("py", "pz")
LANES = 128
SUBLANES = 8
BLOCKS = 2
PAIRED = 0
MOST_PAIRS = 64
VMEM_LIMIT = 56 * 1024 * 1024


def channel_freq(length):
    channel = np.arange(length)
    return np.where(channel == 1, length // 2, channel // 2)


def real_table(length):
    freq = channel_freq(length)
    phase = (freq[:, None] * np.arange(length)[None, :]) % length
    angle = 2.0 * np.pi / length * phase
    odd = (np.arange(length) % 2 == 1) & (np.arange(length) > 1)
    single = np.arange(length) < 2
    table = np.where(odd[:, None], np.sin(angle), np.cos(angle))
    return (table * np.sqrt(np.where(single, 1.0, 2.0) / length)[:, None]).astype(np.float32)


def axis_terms(freq, length):
    scaled = freq / length
    return (scaled**2).astype(np.float32), ((4.0 + 2.0 * np.cos(2.0 * np.pi * scaled)) / 6.0).astype(np.float32)


def radial_body(coef_ref, x_ref, y_ref, z_ref, *out_refs):
    r = pl.program_id(0)
    count = coef_ref.shape[0] // 4
    _, y_count, z_count = out_refs[0].shape
    chunk = min(2 * SUBLANES, y_count)
    z_square, z_smooth = z_ref[0:1], z_ref[1:2]

    def rows(step, carry):
        part = pl.ds(step * chunk, chunk)
        ratio = 4.0 * (y_ref[0, part] + x_ref[0, r] + z_square) / 3.0
        volume = ratio * jnp.sqrt(ratio)
        total = [jnp.zeros((chunk, z_count), jnp.float32) for _ in range(4)]
        for index in range(count):
            basis = jnp.exp(-jnp.square((volume - (index + 0.5) / count) * count))
            total = [value + coef_ref[n * count + index] * basis for n, value in enumerate(total)]
        smooth = y_ref[1, part] * x_ref[1, r] * z_smooth
        for value, ref in zip(total, out_refs):
            ref[0, part] = value * smooth
        return carry

    lax.fori_loop(0, y_count // chunk, rows, 0)


def radial_kernel(coef, x_terms, y_freq, z_freq):
    y_count, z_count = y_freq.size, z_freq.size
    rows = x_terms.shape[1]
    y_terms = jnp.asarray(np.stack(axis_terms(y_freq, y_count))[:, :, None])
    z_terms = jnp.asarray(np.stack(axis_terms(z_freq, z_count)))
    scalars = pl.BlockSpec(memory_space=pltpu.SMEM)
    return pl.pallas_call(
        radial_body,
        grid=(rows,),
        in_specs=[
            scalars,
            scalars,
            pl.BlockSpec(y_terms.shape, lambda r: (0, 0, 0)),
            pl.BlockSpec(z_terms.shape, lambda r: (0, 0)),
        ],
        out_specs=[pl.BlockSpec((1, y_count, z_count), lambda r: (r, 0, 0))] * 4,
        out_shape=[jax.ShapeDtypeStruct((rows, y_count, z_count), jnp.float32)] * 4,
        compiler_params=params(),
        name="radial_kernel",
    )(coef.reshape(-1), x_terms, y_terms, z_terms)


def dot(left, right, left_dim, right_dim):
    dims = (((left_dim,), (right_dim,)), ((), ()))
    return lax.dot_general(left, right, dims, precision=HIGH, preferred_element_type=jnp.float32)


def params():
    return pltpu.CompilerParams(vmem_limit_bytes=VMEM_LIMIT)


def x_groups(x_count, world):
    table, freq = real_table(x_count), channel_freq(x_count)
    if x_count // world % (2 * SUBLANES) or x_count // 2 % LANES:
        return [(table, 0, freq)]
    half = x_count // 2
    return [(table[freq % 2 == odd][:, :half], 1 - 2 * odd, freq[freq % 2 == odd]) for odd in range(2)]


def place_table(base_ref, table_ref, placed):
    @pl.when(pl.program_id(0) == 0)
    def _():
        for k in range(placed.shape[0]):
            placed[k] = table_ref[k ^ base_ref[0]]

    world, rows, width = placed.shape
    return placed[...].reshape(world * rows, width)


def x_forward_body(sign, base_ref, table_ref, one_ref, two_ref, out_ref, placed):
    world, _, rows, cells = out_ref.shape
    table = place_table(base_ref, table_ref, placed)
    for a, ref in enumerate((one_ref, two_ref)):
        values = ref[...].reshape(cells, ref.shape[-1])
        if sign:
            half = values.shape[1] // 2
            values = values[:, :half] + values[:, half:] if sign > 0 else values[:, :half] - values[:, half:]
        out_ref[:, a] = dot(table, values, 1, 1).reshape(world, rows, cells)


def cell_blocks(y_local, z_local):
    blocks = BLOCKS
    while y_local % blocks or (y_local // blocks * z_local) % LANES:
        blocks //= 2
    return blocks


def x_forward(base, table, sign, fields):
    y_local, z_local, x_count = fields[0].shape
    world, rows, _ = table.shape
    blocks = cell_blocks(y_local, z_local)
    part = y_local // blocks
    field_spec = pl.BlockSpec((part, z_local, x_count), lambda i: (i, 0, 0))
    return pl.pallas_call(
        functools.partial(x_forward_body, sign),
        grid=(blocks,),
        in_specs=[
            pl.BlockSpec(memory_space=pltpu.SMEM),
            pl.BlockSpec(table.shape, lambda i: (0, 0, 0)),
            field_spec,
            field_spec,
        ],
        out_specs=pl.BlockSpec((world, 2, rows, part * z_local), lambda i: (0, 0, 0, i)),
        out_shape=jax.ShapeDtypeStruct((world, 2, rows, y_local * z_local), jnp.float32),
        scratch_shapes=[pltpu.VMEM(table.shape, jnp.float32)],
        compiler_params=params(),
        name="x_forward",
    )(base, table, *fields)


def x_inverse_body(base_ref, table_ref, value_ref, *refs):
    *refs, placed = refs
    table = place_table(base_ref, table_ref, placed)
    for a, out_ref in enumerate(refs[-2:]):
        world, _, rows, cells = value_ref.shape
        value = value_ref[:, a].reshape(world * rows, cells)
        total = dot(value, table, 0, 0)
        if len(refs) == 4:
            even = refs[a][...].reshape(total.shape)
            total = jnp.concatenate([even + total, even - total], axis=1)
        out_ref[...] = total.reshape(out_ref.shape)


def x_inverse(base, table, value, even, y_local, z_local):
    world, _, rows, _ = value.shape
    width = table.shape[2]
    blocks = cell_blocks(y_local, z_local)
    part = y_local // blocks
    block = lambda count: pl.BlockSpec((part, z_local, count), lambda i: (i, 0, 0))
    x_count = 2 * width if even else width
    out = jax.ShapeDtypeStruct((y_local, z_local, x_count), jnp.float32)
    return pl.pallas_call(
        x_inverse_body,
        grid=(blocks,),
        in_specs=[
            pl.BlockSpec(memory_space=pltpu.SMEM),
            pl.BlockSpec(table.shape, lambda i: (0, 0, 0)),
            pl.BlockSpec((world, 2, rows, part * z_local), lambda i: (0, 0, 0, i)),
        ]
        + [block(width)] * len(even),
        out_specs=(block(x_count), block(x_count)),
        out_shape=(out, out),
        scratch_shapes=[pltpu.VMEM(table.shape, jnp.float32)],
        compiler_params=params(),
        name="x_inverse",
    )(base, table, value, *even)


def swap_groups(values, width):
    values = list(values)
    count = len(values)
    lane = lax.broadcasted_iota(jnp.int32, values[0].shape, 1)
    step = 1
    while step < count:
        low = (lane // (step * width)) % 2 == 0
        for m in range(count):
            if m & step == 0:
                one, two = values[m], values[m | step]
                values[m] = jnp.where(low, one, pltpu.roll(two, step * width, 1))
                values[m | step] = jnp.where(low, pltpu.roll(one, LANES - step * width, 1), two)
        step *= 2
    return values


def yz_body(pz, base_ref, value_ref, y_ref, z_ref, k00, k01, k10, k11, out_ref, scratch):
    world, _, rows, cells = value_ref.shape
    py = world // pz
    y_count = y_ref.shape[0]
    z_count = z_ref.shape[0]
    z_local = z_count // pz
    base = base_ref[0]
    split = LANES // z_local
    tiles = cells // LANES
    block = split * tiles * rows
    halves = z_count // LANES
    r = pl.program_id(0)

    @pl.when(r == 0)
    def _():
        for a in range(2):

            def forward(i, carry):
                spread = []
                for high in range(pz // split):
                    group = []
                    for low in range(split):
                        value = value_ref[(i * pz + high * split + low) ^ base, a]
                        group.append(
                            jnp.concatenate([value[:, t * LANES : (t + 1) * LANES] for t in range(tiles)], axis=0)
                        )
                    spread.append(swap_groups(group, z_local))
                lines = [jnp.concatenate([part[p] for part in spread], axis=1) for p in range(split)]
                lines = jnp.concatenate(lines, axis=0)
                lines = dot(lines, z_ref[...], 1, 1)
                for t in range(halves):
                    scratch[a, t, pl.ds(i * block, block), :] = lines[:, t * LANES : (t + 1) * LANES]
                return carry

            lax.fori_loop(0, py, forward, 0)

    spectra = []
    for a in range(2):
        plane = [scratch[a, t, pl.ds(r, y_count, stride=rows), :] for t in range(halves)]
        spectra.append(dot(y_ref[...], jnp.concatenate(plane, axis=1), 1, 0))
    for a, (first, second) in enumerate(((k00, k01), (k10, k11))):
        weighed = first[0] * spectra[0] + second[0] * spectra[1]
        plane = dot(y_ref[...], weighed, 0, 0)
        for t in range(halves):
            scratch[a, t, pl.ds(r, y_count, stride=rows), :] = plane[:, t * LANES : (t + 1) * LANES]

    @pl.when(r == rows - 1)
    def _():
        for a in range(2):

            def backward(i, carry):
                lines = [scratch[a, t, pl.ds(i * block, block), :] for t in range(halves)]
                lines = dot(jnp.concatenate(lines, axis=1), z_ref[...], 1, 0)
                size = block // split
                for high in range(pz // split):
                    lanes = slice(high * LANES, (high + 1) * LANES)
                    group = swap_groups([lines[p * size : (p + 1) * size, lanes] for p in range(split)], z_local)
                    for low in range(split):
                        slot = (i * pz + high * split + low) ^ base
                        for t in range(tiles):
                            piece = group[low][t * rows : (t + 1) * rows]
                            out_ref[slot, a, :, t * LANES : (t + 1) * LANES] = piece
                return carry

            lax.fori_loop(0, py, backward, 0)


def yz_apply(base, value, kernel, sizes):
    py, pz, y_local, z_local = sizes
    _, _, rows, cells = value.shape
    y_count, z_count = py * y_local, pz * z_local
    y_table, z_table = real_table(y_count), jnp.asarray(real_table(z_count))
    if rows % SUBLANES or LANES % z_local or cells % LANES or z_count % LANES or pz % (LANES // z_local):
        return yz_plain(value, kernel, sizes, jnp.asarray(y_table), z_table)
    split = LANES // z_local
    order = np.arange(y_count).reshape(py, y_local // split, split).transpose(0, 2, 1).reshape(-1)
    y_table = jnp.asarray(y_table[:, order])
    whole = lambda shape: pl.BlockSpec(shape, lambda r: (0,) * len(shape))
    k_spec = pl.BlockSpec((1, y_count, z_count), lambda r: (r, 0, 0))
    return pl.pallas_call(
        functools.partial(yz_body, pz),
        grid=(rows,),
        in_specs=[pl.BlockSpec(memory_space=pltpu.SMEM), whole(value.shape), whole(y_table.shape), whole(z_table.shape)] + [k_spec] * 4,
        out_specs=whole(value.shape),
        out_shape=jax.ShapeDtypeStruct(value.shape, jnp.float32),
        scratch_shapes=[pltpu.VMEM((2, z_count // LANES, y_count * rows, LANES), jnp.float32)],
        compiler_params=params(),
        name="yz_apply",
    )(base, value, y_table, z_table, *kernel)


def yz_plain(value, kernel, sizes, y_table, z_table):
    py, pz, y_local, z_local = sizes
    rows = value.shape[2]
    value = value.reshape(py, pz, 2, rows, y_local, z_local).transpose(2, 3, 0, 4, 1, 5)
    value = value.reshape(2, rows, py * y_local, pz * z_local)
    value = jnp.einsum("aryz,mz->arym", value, z_table, precision=HIGH)
    value = jnp.einsum("arym,ky->arkm", value, y_table, precision=HIGH)
    k00, k01, k10, k11 = kernel
    value = jnp.stack([k00 * value[0] + k01 * value[1], k10 * value[0] + k11 * value[1]])
    value = jnp.einsum("arkm,ky->arym", value, y_table, precision=HIGH)
    value = jnp.einsum("arym,mz->aryz", value, z_table, precision=HIGH)
    value = value.reshape(2, rows, py, y_local, pz, z_local).transpose(2, 4, 0, 1, 3, 5)
    return value.reshape(py * pz, 2, rows, y_local * z_local)


def shards(field_one, field_two, coef):
    y_local, z_local, x_count = field_one.shape
    py_count = lax.axis_size("py")
    pz_count = lax.axis_size("pz")
    sizes = (py_count, pz_count, y_local, z_local)
    y_count = y_local * py_count
    z_count = z_local * pz_count
    world = py_count * pz_count
    me = lax.axis_index("py") * pz_count + lax.axis_index("pz")
    freq_y, freq_z = channel_freq(y_count), channel_freq(z_count)
    fields = (field_one, field_two)
    groups = x_groups(x_count, world)

    def all_at_once(value):
        return lax.all_to_all(value, AXES, split_axis=0, concat_axis=0, tiled=True)

    def by_pairs(value):
        parts = [value[:1]]
        for k in range(1, world):
            pairs = [(i, i ^ k) for i in range(world)]
            parts.append(lax.ppermute(value[k : k + 1], AXES, pairs))
        return jnp.concatenate(parts, axis=0)

    paired = len(groups) == 2 and world & (world - 1) == 0 and world <= MOST_PAIRS
    plans = []
    for index, (table, sign, freq) in enumerate(groups):
        rows = freq.size // world
        x_terms = jnp.asarray(np.stack(axis_terms(freq, x_count)))
        x_terms = lax.dynamic_slice_in_dim(x_terms, me * rows, rows, axis=1)
        relative = paired and index == PAIRED
        base = jnp.reshape(me if relative else jnp.zeros_like(me), (1,))
        table = jnp.asarray(table.reshape(world, rows, -1))
        plans.append((base, table, sign, x_terms, by_pairs if relative else all_at_once))

    arrived = []
    for base, table, sign, _, exchange in plans:
        arrived.append(exchange(x_forward(base, table, sign, fields)))
    returned = []
    for value, (base, _, _, x_terms, exchange) in zip(arrived, plans):
        kernel = radial_kernel(coef, x_terms, freq_y, freq_z)
        value = yz_apply(base, value, kernel, sizes)
        returned.append(exchange(value))
    results = ()
    for value, (base, table, _, _, _) in zip(returned, plans):
        results = x_inverse(base, table, value, results, y_local, z_local)
    return tuple(results)


def solution(mesh):
    in_specs = (P("py", "pz", None), P("py", "pz", None), P())
    out_specs = (P("py", "pz", None), P("py", "pz", None))
    return jax.shard_map(shards, mesh=mesh, in_specs=in_specs, out_specs=out_specs, check_vma=False)
```

```python
import functools

import jax
import jax.numpy as jnp
import numpy as np
from jax import lax
from jax.experimental import pallas as pl
from jax.experimental.pallas import tpu as pltpu
from jax.sharding import PartitionSpec as P


HIGH = lax.Precision.HIGHEST
AXES = ("py", "pz")
LANES = 128
SUBLANES = 8
BLOCKS = 2
PAIRED = 0
MOST_PAIRS = 64
EARLY = 4
VMEM_LIMIT = 56 * 1024 * 1024


def channel_freq(length):
    channel = np.arange(length)
    return np.where(channel == 1, length // 2, channel // 2)


def real_table(length):
    freq = channel_freq(length)
    phase = (freq[:, None] * np.arange(length)[None, :]) % length
    angle = 2.0 * np.pi / length * phase
    odd = (np.arange(length) % 2 == 1) & (np.arange(length) > 1)
    single = np.arange(length) < 2
    table = np.where(odd[:, None], np.sin(angle), np.cos(angle))
    return (table * np.sqrt(np.where(single, 1.0, 2.0) / length)[:, None]).astype(np.float32)


def axis_terms(freq, length):
    scaled = freq / length
    return (scaled**2).astype(np.float32), ((4.0 + 2.0 * np.cos(2.0 * np.pi * scaled)) / 6.0).astype(np.float32)


def radial_body(coef_ref, x_ref, y_ref, z_ref, *out_refs):
    r = pl.program_id(0)
    count = coef_ref.shape[0] // 4
    _, y_count, z_count = out_refs[0].shape
    chunk = min(2 * SUBLANES, y_count)
    z_square, z_smooth = z_ref[0:1], z_ref[1:2]

    def rows(step, carry):
        part = pl.ds(step * chunk, chunk)
        ratio = 4.0 * (y_ref[0, part] + x_ref[0, r] + z_square) / 3.0
        volume = ratio * jnp.sqrt(ratio)
        total = [jnp.zeros((chunk, z_count), jnp.float32) for _ in range(4)]
        for index in range(count):
            basis = jnp.exp(-jnp.square((volume - (index + 0.5) / count) * count))
            total = [value + coef_ref[n * count + index] * basis for n, value in enumerate(total)]
        smooth = y_ref[1, part] * x_ref[1, r] * z_smooth
        for value, ref in zip(total, out_refs):
            ref[0, part] = value * smooth
        return carry

    lax.fori_loop(0, y_count // chunk, rows, 0)


def radial_kernel(coef, x_terms, y_freq, z_freq):
    y_count, z_count = y_freq.size, z_freq.size
    rows = x_terms.shape[1]
    y_terms = jnp.asarray(np.stack(axis_terms(y_freq, y_count))[:, :, None])
    z_terms = jnp.asarray(np.stack(axis_terms(z_freq, z_count)))
    scalars = pl.BlockSpec(memory_space=pltpu.SMEM)
    return pl.pallas_call(
        radial_body,
        grid=(rows,),
        in_specs=[
            scalars,
            scalars,
            pl.BlockSpec(y_terms.shape, lambda r: (0, 0, 0)),
            pl.BlockSpec(z_terms.shape, lambda r: (0, 0)),
        ],
        out_specs=[pl.BlockSpec((1, y_count, z_count), lambda r: (r, 0, 0))] * 4,
        out_shape=[jax.ShapeDtypeStruct((rows, y_count, z_count), jnp.float32)] * 4,
        compiler_params=params(),
        name="radial_kernel",
    )(coef.reshape(-1), x_terms, y_terms, z_terms)


def dot(left, right, left_dim, right_dim):
    dims = (((left_dim,), (right_dim,)), ((), ()))
    return lax.dot_general(left, right, dims, precision=HIGH, preferred_element_type=jnp.float32)


def in_halves(value):
    high = value.astype(jnp.bfloat16)
    return high, (value - high.astype(jnp.float32)).astype(jnp.bfloat16)


def dot_in_halves(left, right, left_dim, right_dim):
    dims = (((left_dim,), (right_dim,)), ((), ()))
    mul = lambda one, two: lax.dot_general(one, two, dims, preferred_element_type=jnp.float32)
    (left_high, left_low), (right_high, right_low) = in_halves(left), in_halves(right)
    return mul(left_high, right_high) + (mul(left_high, right_low) + mul(left_low, right_high))


def params():
    return pltpu.CompilerParams(vmem_limit_bytes=VMEM_LIMIT)


def x_groups(x_count, world):
    table, freq = real_table(x_count), channel_freq(x_count)
    if x_count // world % (2 * SUBLANES) or x_count // 2 % LANES:
        return [(table, 0, freq)]
    half = x_count // 2
    return [(table[freq % 2 == odd][:, :half], 1 - 2 * odd, freq[freq % 2 == odd]) for odd in range(2)]


def place_table(base_ref, table_ref, slots, placed):
    @pl.when(pl.program_id(0) == 0)
    def _():
        for n, k in enumerate(slots):
            placed[n] = table_ref[k ^ base_ref[0]]

    world, rows, width = placed.shape
    return placed[...].reshape(world * rows, width)


def x_forward_body(sign, slots, base_ref, table_ref, one_ref, two_ref, *refs):
    *outs, placed = refs
    table = place_table(base_ref, table_ref, slots, placed)
    for a, ref in enumerate((one_ref, two_ref)):
        values = ref[...].reshape(-1, ref.shape[-1])
        if sign:
            half = values.shape[1] // 2
            values = values[:, :half] + values[:, half:] if sign > 0 else values[:, :half] - values[:, half:]
        spectrum = dot(table, values, 1, 1)
        for n, out_ref in enumerate(outs):
            count, _, rows, cells = out_ref.shape
            size = count * rows
            out_ref[:, a] = spectrum[n * size : (n + 1) * size].reshape(count, rows, cells)


def cell_blocks(y_local, z_local):
    blocks = BLOCKS
    while y_local % blocks or (y_local // blocks * z_local) % LANES:
        blocks //= 2
    return blocks


def x_forward(base, slots, table, sign, fields, pieces):
    y_local, z_local, x_count = fields[0].shape
    _, rows, width = table.shape
    blocks = cell_blocks(y_local, z_local)
    part = y_local // blocks
    count = len(slots) // pieces
    field_spec = pl.BlockSpec((part, z_local, x_count), lambda i: (i, 0, 0))
    out = jax.ShapeDtypeStruct((count, 2, rows, y_local * z_local), jnp.float32)
    return pl.pallas_call(
        functools.partial(x_forward_body, sign, slots),
        grid=(blocks,),
        in_specs=[
            pl.BlockSpec(memory_space=pltpu.SMEM),
            pl.BlockSpec(table.shape, lambda i: (0, 0, 0)),
            field_spec,
            field_spec,
        ],
        out_specs=[pl.BlockSpec((count, 2, rows, part * z_local), lambda i: (0, 0, 0, i))] * pieces,
        out_shape=[out] * pieces,
        scratch_shapes=[pltpu.VMEM((len(slots), rows, width), jnp.float32)],
        compiler_params=params(),
        name="x_forward",
    )(base, table, *fields)


def x_inverse_body(slots, base_ref, table_ref, value_ref, *refs):
    *refs, placed = refs
    table = place_table(base_ref, table_ref, slots, placed)
    for a, out_ref in enumerate(refs[-2:]):
        world, _, rows, cells = value_ref.shape
        value = value_ref[:, a].reshape(world * rows, cells)
        if len(refs) == 4:
            total = dot_in_halves(value, table, 0, 0)
            even = refs[a][...].reshape(total.shape)
            total = jnp.concatenate([even + total, even - total], axis=1)
        else:
            total = dot(value, table, 0, 0)
        out_ref[...] = total.reshape(out_ref.shape)


def x_inverse(base, slots, table, value, even, y_local, z_local):
    world, _, rows, _ = value.shape
    width = table.shape[2]
    blocks = cell_blocks(y_local, z_local)
    part = y_local // blocks
    block = lambda count: pl.BlockSpec((part, z_local, count), lambda i: (i, 0, 0))
    x_count = 2 * width if even else width
    out = jax.ShapeDtypeStruct((y_local, z_local, x_count), jnp.float32)
    return pl.pallas_call(
        functools.partial(x_inverse_body, slots),
        grid=(blocks,),
        in_specs=[
            pl.BlockSpec(memory_space=pltpu.SMEM),
            pl.BlockSpec(table.shape, lambda i: (0, 0, 0)),
            pl.BlockSpec((world, 2, rows, part * z_local), lambda i: (0, 0, 0, i)),
        ]
        + [block(width)] * len(even),
        out_specs=(block(x_count), block(x_count)),
        out_shape=(out, out),
        scratch_shapes=[pltpu.VMEM(table.shape, jnp.float32)],
        compiler_params=params(),
        name="x_inverse",
    )(base, table, value, *even)


def swap_groups(values, width):
    values = list(values)
    count = len(values)
    lane = lax.broadcasted_iota(jnp.int32, values[0].shape, 1)
    step = 1
    while step < count:
        low = (lane // (step * width)) % 2 == 0
        for m in range(count):
            if m & step == 0:
                one, two = values[m], values[m | step]
                values[m] = jnp.where(low, one, pltpu.roll(two, step * width, 1))
                values[m | step] = jnp.where(low, pltpu.roll(one, LANES - step * width, 1), two)
        step *= 2
    return values


def yz_body(pz, base_ref, place_ref, value_ref, y_ref, z_ref, k00, k01, k10, k11, out_ref, scratch):
    world, _, rows, cells = value_ref.shape
    py = world // pz
    y_count = y_ref.shape[0]
    z_count = z_ref.shape[0]
    z_local = z_count // pz
    split = LANES // z_local
    tiles = cells // LANES
    block = split * tiles * rows
    halves = z_count // LANES
    r = pl.program_id(0)

    @pl.when(r == 0)
    def _():
        for a in range(2):

            def forward(i, carry):
                spread = []
                for high in range(pz // split):
                    group = []
                    for low in range(split):
                        value = value_ref[place_ref[(i * pz + high * split + low) ^ base_ref[0]], a]
                        group.append(
                            jnp.concatenate([value[:, t * LANES : (t + 1) * LANES] for t in range(tiles)], axis=0)
                        )
                    spread.append(swap_groups(group, z_local))
                lines = [jnp.concatenate([part[p] for part in spread], axis=1) for p in range(split)]
                lines = jnp.concatenate(lines, axis=0)
                lines = dot(lines, z_ref[...], 1, 1)
                for t in range(halves):
                    scratch[a, t, pl.ds(i * block, block), :] = lines[:, t * LANES : (t + 1) * LANES]
                return carry

            lax.fori_loop(0, py, forward, 0)

    spectra = []
    for a in range(2):
        plane = [scratch[a, t, pl.ds(r, y_count, stride=rows), :] for t in range(halves)]
        spectra.append(dot(y_ref[...], jnp.concatenate(plane, axis=1), 1, 0))
    for a, (first, second) in enumerate(((k00, k01), (k10, k11))):
        weighed = first[0] * spectra[0] + second[0] * spectra[1]
        plane = dot(y_ref[...], weighed, 0, 0)
        for t in range(halves):
            scratch[a, t, pl.ds(r, y_count, stride=rows), :] = plane[:, t * LANES : (t + 1) * LANES]

    @pl.when(r == rows - 1)
    def _():
        for a in range(2):

            def backward(i, carry):
                lines = [scratch[a, t, pl.ds(i * block, block), :] for t in range(halves)]
                lines = dot(jnp.concatenate(lines, axis=1), z_ref[...], 1, 0)
                size = block // split
                for high in range(pz // split):
                    lanes = slice(high * LANES, (high + 1) * LANES)
                    group = swap_groups([lines[p * size : (p + 1) * size, lanes] for p in range(split)], z_local)
                    for low in range(split):
                        slot = place_ref[(i * pz + high * split + low) ^ base_ref[0]]
                        for t in range(tiles):
                            piece = group[low][t * rows : (t + 1) * rows]
                            out_ref[slot, a, :, t * LANES : (t + 1) * LANES] = piece
                return carry

            lax.fori_loop(0, py, backward, 0)


def yz_apply(base, slots, value, kernel, sizes):
    py, pz, y_local, z_local = sizes
    _, _, rows, cells = value.shape
    y_count, z_count = py * y_local, pz * z_local
    y_table, z_table = real_table(y_count), jnp.asarray(real_table(z_count))
    if rows % SUBLANES or LANES % z_local or cells % LANES or z_count % LANES or pz % (LANES // z_local):
        return yz_plain(value, kernel, sizes, jnp.asarray(y_table), z_table)
    split = LANES // z_local
    order = np.arange(y_count).reshape(py, y_local // split, split).transpose(0, 2, 1).reshape(-1)
    y_table = jnp.asarray(y_table[:, order])
    whole = lambda shape: pl.BlockSpec(shape, lambda r: (0,) * len(shape))
    k_spec = pl.BlockSpec((1, y_count, z_count), lambda r: (r, 0, 0))
    return pl.pallas_call(
        functools.partial(yz_body, pz),
        grid=(rows,),
        in_specs=[pl.BlockSpec(memory_space=pltpu.SMEM)] * 2 + [whole(value.shape), whole(y_table.shape), whole(z_table.shape)] + [k_spec] * 4,
        out_specs=whole(value.shape),
        out_shape=jax.ShapeDtypeStruct(value.shape, jnp.float32),
        scratch_shapes=[pltpu.VMEM((2, z_count // LANES, y_count * rows, LANES), jnp.float32)],
        compiler_params=params(),
        name="yz_apply",
    )(base, jnp.asarray(np.argsort(slots).astype(np.int32)), value, y_table, z_table, *kernel)


def yz_plain(value, kernel, sizes, y_table, z_table):
    py, pz, y_local, z_local = sizes
    rows = value.shape[2]
    value = value.reshape(py, pz, 2, rows, y_local, z_local).transpose(2, 3, 0, 4, 1, 5)
    value = value.reshape(2, rows, py * y_local, pz * z_local)
    value = jnp.einsum("aryz,mz->arym", value, z_table, precision=HIGH)
    value = jnp.einsum("arym,ky->arkm", value, y_table, precision=HIGH)
    k00, k01, k10, k11 = kernel
    value = jnp.stack([k00 * value[0] + k01 * value[1], k10 * value[0] + k11 * value[1]])
    value = jnp.einsum("arkm,ky->arym", value, y_table, precision=HIGH)
    value = jnp.einsum("arym,mz->aryz", value, z_table, precision=HIGH)
    value = value.reshape(2, rows, py, y_local, pz, z_local).transpose(2, 4, 0, 1, 3, 5)
    return value.reshape(py * pz, 2, rows, y_local * z_local)


def shards(field_one, field_two, coef):
    y_local, z_local, x_count = field_one.shape
    py_count = lax.axis_size("py")
    pz_count = lax.axis_size("pz")
    sizes = (py_count, pz_count, y_local, z_local)
    y_count = y_local * py_count
    z_count = z_local * pz_count
    world = py_count * pz_count
    me = lax.axis_index("py") * pz_count + lax.axis_index("pz")
    freq_y, freq_z = channel_freq(y_count), channel_freq(z_count)
    fields = (field_one, field_two)
    groups = x_groups(x_count, world)

    def all_at_once(value):
        return lax.all_to_all(value, AXES, split_axis=0, concat_axis=0, tiled=True)

    def swap(value, k):
        return value if k == 0 else lax.ppermute(value, AXES, [(i, i ^ k) for i in range(world)])

    paired = len(groups) == 2 and world & (world - 1) == 0 and 2 * EARLY <= world <= MOST_PAIRS
    by_distance = sorted(range(world), key=lambda k: (k & (pz_count // 2) == 0, k == 0, k))
    plans = []
    for index, (table, sign, freq) in enumerate(groups):
        rows = freq.size // world
        x_terms = jnp.asarray(np.stack(axis_terms(freq, x_count)))
        x_terms = lax.dynamic_slice_in_dim(x_terms, me * rows, rows, axis=1)
        relative = paired and index == PAIRED
        slots = by_distance if relative else list(range(world))
        base = jnp.reshape(me if relative else jnp.zeros_like(me), (1,))
        plans.append((base, slots, jnp.asarray(table.reshape(world, rows, -1)), sign, x_terms, relative))

    arrived = []
    for base, slots, table, sign, _, relative in plans:
        if relative:
            values = []
            for some in (slots[:EARLY], slots[EARLY:]):
                sent = x_forward(base, some, table, sign, fields, len(some))
                values += [swap(value, k) for value, k in zip(sent, some)]
            arrived.append(jnp.concatenate(values, axis=0))
        else:
            (sent,) = x_forward(base, slots, table, sign, fields, 1)
            arrived.append(all_at_once(sent))
    returned = []
    for value, (base, slots, _, _, x_terms, relative) in zip(arrived, plans):
        kernel = radial_kernel(coef, x_terms, freq_y, freq_z)
        value = yz_apply(base, slots, value, kernel, sizes)
        if relative:
            values = [swap(value[n : n + 1], k) for n, k in enumerate(slots)]
            returned.append(jnp.concatenate(values, axis=0))
        else:
            returned.append(all_at_once(value))
    results = ()
    for value, (base, slots, table, _, _, _) in zip(returned, plans):
        results = x_inverse(base, slots, table, value, results, y_local, z_local)
    return tuple(results)


def solution(mesh):
    in_specs = (P("py", "pz", None), P("py", "pz", None), P())
    out_specs = (P("py", "pz", None), P("py", "pz", None))
    return jax.shard_map(shards, mesh=mesh, in_specs=in_specs, out_specs=out_specs, check_vma=False)
```
